32 devices in a mesh: seq: 16 (over z, y, x), fsdp: 2 (over core).
Axes of the slice: x: 2, y: 2, z: 4, core: 2. Of those that a mesh axis runs over, the one named last changes fastest.
Arguments:
- tokens: bfloat16 [2, 4096, 1024], P('fsdp', 'seq'), may hold values from -6 to 6
- segment_ids: int32 [2, 4096], P('fsdp'), may hold values from 0 to 5, never falling along the last dimension, each value on 1 to 2048 neighbouring positions
- norm_gain: bfloat16 [1024], P('fsdp'), may hold values from 0.25 to 1.75
- qkv_weight: bfloat16 [1024, 3072], P('fsdp'), may hold values from -0.1875 to 0.1875
- proj_weight: bfloat16 [1024, 1024], P('fsdp'), may hold values from -1 to 1
- ffn_gain: bfloat16 [1024], P('fsdp'), may hold values from 0.25 to 1.75
- wide_weight: bfloat16 [1024, 5248], P('fsdp'), may hold values from -0.1875 to 0.1875
- narrow_weight: bfloat16 [2624, 1024], P(None, 'fsdp'), may hold values from -0.15625 to 0.15625
- cotangent: bfloat16 [2, 4096, 1024], P('fsdp', 'seq'), may hold values from -6 to 6
Outputs:
- mixed: bfloat16 [2, 4096, 1024], P('fsdp', 'seq')
- tokens_grad: bfloat16 [2, 4096, 1024], P('fsdp', 'seq')
- norm_gain_grad: float32 [1024], P(('seq', 'fsdp'))
- qkv_grad: float32 [1024, 3072], P(('seq', 'fsdp'))
- proj_grad: float32 [1024, 1024], P(('seq', 'fsdp'))
- ffn_gain_grad: float32 [1024], P(('seq', 'fsdp'))
- wide_grad: float32 [1024, 5248], P(('seq', 'fsdp'))
- narrow_grad: float32 [2624, 1024], P(None, ('seq', 'fsdp'))
The draws below stay inside these ranges and needn't reach their ends.
Inputs may be any that keep to these rules, and one draw needn't show every extreme that they name: `segment_ids`: in each stream the ids start at 0 and never fall; each of the 6 segments holds 1 to 2048 tokens, and one holds exactly 2048.
All inputs are finite; a program needn't handle non-finite values.
Results may differ from the reference program's by a relative error of at most 0.015.
Values may be sent and summed in bfloat16 or wider, within the bound.
A program may use at most 256 MiB of HBM per device.

```python
import math
import jax
import jax.numpy as jnp
import numpy as np
from jax import lax

D = 1024
HEAD_DIM = 64
FF = 2624
HALF_WIN = 64
STREAMS = 2
LEN = 4096
SEG_MOST = 2048
SEGS = 6


def with_spikes(result, key, source, target, blocks, factor):
    def block_of(position):
        return (jnp.arange(result.shape[position]) // (result.shape[position] // blocks)).reshape((-1,) + (1,) * (result.ndim - 1 - position))

    first = jax.random.permutation(key, blocks)[block_of(target)]
    other_side = (block_of(target) + blocks // 2) % blocks
    return jnp.where((block_of(source) == first) | (block_of(source) == other_side), factor * result, result)


def block_levels(stream_key, extent, cuts, smallest, high):
    def one(position, blocks):
        heights = jax.random.uniform(jax.random.fold_in(jax.random.fold_in(stream_key, 6), position), (blocks,), jnp.float32, smallest / len(cuts), high / len(cuts))
        return jnp.repeat(jnp.exp(heights), extent[position] // blocks).reshape((-1,) + (1,) * (len(extent) - position - 1))

    level = one(*cuts[0])
    for cut in cuts[1:]:
        level = level * one(*cut)
    return level


def split_up(count, total, most, lean):
    weights = [(1 << 20) // math.isqrt(standing ** lean) + 1 for standing in range(2, count + 1)]
    spare, given = total - most - (count - 1), [1] * (count - 1)
    while spare > 0:
        free = [i for i in range(count - 1) if given[i] < most]
        pool, remaining = sum([weights[i] for i in free]), spare
        for i in free:
            addition = min(most - given[i], max(1, remaining * weights[i] // pool), spare)
            given[i] = given[i] + addition
            spare = spare - addition
    return np.array([most] + given)


def ragged(stream_key, number_of, total, limit, lean):
    if number_of == 2:
        one = jax.random.randint(stream_key, (), max(1, total - limit), min(limit, total - 1) + 1)
        return jnp.stack([one, total - one])
    tallies = jnp.asarray(split_up(number_of, total, limit, lean), jnp.int32)
    pairs = (number_of - 1) // 2
    source_of, taker = tallies[1:1 + 2 * pairs:2], tallies[2:2 + 2 * pairs:2]
    margin = jnp.minimum(source_of - 1, limit - taker)
    moved = jax.random.randint(jax.random.fold_in(stream_key, 1), (pairs,), 0, 1 << 20) % (margin + 1)
    tallies = tallies.at[1:1 + 2 * pairs:2].set(source_of - moved).at[2:2 + 2 * pairs:2].set(taker + moved)
    return tallies[jax.random.permutation(jax.random.fold_in(stream_key, 2), number_of)]


def scatter_about(stream_key, dims, width, most, shards=(), kind=jnp.bfloat16):
    drawn = jax.random.normal(stream_key, dims, jnp.float32) * width
    if len(shards) > 0:
        drawn = block_levels(stream_key, dims, shards, -0.22, 0.18) * drawn
    return jnp.clip(drawn, min=-most, max=most).astype(kind)


def heavy_noise(key, dims, width, most, split, heavy, kind=jnp.bfloat16):
    result = width * jax.random.normal(key, dims, jnp.float32)
    if split:
        result = result * block_levels(key, dims, split, -0.22, 0.18)
    return jnp.clip(with_spikes(result, jax.random.fold_in(key, 3), *heavy), -most, most).astype(kind)


def setup_inputs(seed: int = 0) -> dict:
    arg_keys = jax.random.split(jax.random.key(seed), 10)
    tokens = heavy_noise(arg_keys[0], (STREAMS, LEN, D), 1.0, 6.0, ((0, 2), (1, 16)), (1, 2, 16, 2.0))
    segment_ids = jax.vmap(lambda own: jnp.searchsorted(jnp.cumsum(ragged(own, SEGS, LEN, SEG_MOST, 2)), jnp.arange(LEN), side="right"))(jax.random.split(arg_keys[1], STREAMS)).reshape((STREAMS, LEN)).astype(jnp.int32)
    norm_gain = jnp.clip(1.0 + 0.15 * jax.random.normal(arg_keys[2], (D,), jnp.float32), 0.25, 1.75).astype(jnp.bfloat16)
    qkv_weight = scatter_about(arg_keys[3], (D, 3 * D), D ** -0.5, 0.1875, ((0, 2),))
    proj_weight = scatter_about(arg_keys[4], (D, D), (D // 32) ** -0.5, 1.0, ((0, 2),))
    ffn_gain = jnp.clip(1.0 + 0.15 * jax.random.normal(arg_keys[5], (D,), jnp.float32), 0.25, 1.75).astype(jnp.bfloat16)
    wide_weight = scatter_about(arg_keys[6], (D, 2 * FF), D ** -0.5, 0.1875, ((0, 2),))
    narrow_weight = scatter_about(arg_keys[7], (FF, D), (FF // 2) ** -0.5, 0.15625, ((1, 2),))
    cotangent = scatter_about(arg_keys[8], (STREAMS, LEN, D), 1.0, 6.0, ((0, 2), (1, 16)))
    return dict(tokens=tokens, segment_ids=segment_ids, norm_gain=norm_gain, qkv_weight=qkv_weight, proj_weight=proj_weight, ffn_gain=ffn_gain, wide_weight=wide_weight, narrow_weight=narrow_weight, cotangent=cotangent)


@jax.custom_vjp
def low(v):
    return lax.optimization_barrier(v.astype(jnp.bfloat16)).astype(jnp.float32)

@jax.custom_vjp
def low_back(v):
    return v

def low_keep(v):
    return (low(v), None)

def low_pass(kept, grad):
    return (grad,)

def back_keep(v):
    return (v, None)

def back_low(kept, grad):
    return (low(grad),)
low.defvjp(low_keep, low_pass)
low_back.defvjp(back_keep, back_low)
eps_norm = 1e-05
mask_fill = -1e+30

def layer_norm(values_in, gain_vec):
    centre_mean = lax.optimization_barrier(jnp.mean(values_in, axis=-1, keepdims=True))
    centred = values_in - centre_mean
    variance = lax.optimization_barrier(jnp.mean(centred * centred, axis=-1, keepdims=True))
    return centred * lax.rsqrt(variance + eps_norm) * gain_vec

def angle_table(positions, head_size):
    half_size = head_size // 2
    freqs = jnp.exp(jnp.arange(half_size, dtype=jnp.float32) * (-2.0 * math.log(10000.0) / head_size))
    return positions.astype(jnp.float32)[..., None] * freqs

def rotate(tensor, angles):
    half_size = tensor.shape[-1] // 2
    cosine = jnp.cos(angles)[..., None, :]
    sine = jnp.sin(angles)[..., None, :]
    first_half = tensor[..., :half_size]
    second_half = tensor[..., half_size:]
    return jnp.concatenate([first_half * cosine - second_half * sine, second_half * cosine + first_half * sine], axis=-1)

def geglu(gate_part, up_part):
    return jax.nn.gelu(gate_part, approximate=False) * up_part

def reference(tokens, segment_ids, norm_gain, qkv_weight, proj_weight, ffn_gain, wide_weight, narrow_weight, cotangent):
    maximum_precision = lax.Precision.HIGHEST
    stream_count, length, model_width = tokens.shape
    head_count = model_width // HEAD_DIM
    hidden = narrow_weight.shape[0]
    half_span = HALF_WIN
    block_rows = min(512, length)
    block_count = length // block_rows
    scale = HEAD_DIM ** (-0.5)
    first_of = jax.vmap(lambda stream_ids: jnp.searchsorted(stream_ids, stream_ids, side='left'))(segment_ids).astype(jnp.int32)
    positions = jnp.arange(length, dtype=jnp.int32)[None, :] - first_of
    angles = angle_table(positions, HEAD_DIM)
    padded_ids = jnp.concatenate([jnp.full((stream_count, half_span), -1, jnp.int32), segment_ids.astype(jnp.int32), jnp.full((stream_count, half_span), -2, jnp.int32)], axis=1)

    def attend(queries, keys, values):
        pad_widths = ((0, 0), (half_span, half_span), (0, 0), (0, 0))
        keys_pad = jnp.pad(keys, pad_widths)
        values_pad = jnp.pad(values, pad_widths)

        def one_block(flat_index):
            stream_index = flat_index // block_count
            block_index = flat_index % block_count
            row_start = (block_index * block_rows).astype(jnp.int32)
            zero = jnp.zeros((), jnp.int32)
            query_block = lax.dynamic_slice(queries, (stream_index, row_start, zero, zero), (1, block_rows, head_count, HEAD_DIM))[0]
            key_block = lax.dynamic_slice(keys_pad, (stream_index, row_start, zero, zero), (1, block_rows + 2 * half_span, head_count, HEAD_DIM))[0]
            value_block = lax.dynamic_slice(values_pad, (stream_index, row_start, zero, zero), (1, block_rows + 2 * half_span, head_count, HEAD_DIM))[0]
            query_ids = lax.dynamic_slice(segment_ids.astype(jnp.int32), (stream_index, row_start), (1, block_rows))[0]
            key_ids = lax.dynamic_slice(padded_ids, (stream_index, row_start), (1, block_rows + 2 * half_span))[0]
            query_place = row_start + jnp.arange(block_rows, dtype=jnp.int32)
            key_place = row_start - half_span + jnp.arange(block_rows + 2 * half_span, dtype=jnp.int32)
            allowed = (jnp.abs(query_place[:, None] - key_place[None, :]) <= half_span) & (query_ids[:, None] == key_ids[None, :])
            scores = low_back(jnp.einsum('qhd,khd->hqk', query_block, key_block, precision=maximum_precision) * scale)
            scores = jnp.where(allowed[None], scores, mask_fill)
            probs = jax.nn.softmax(scores, axis=-1)
            return jnp.einsum('hqk,khd->qhd', low(probs), value_block, precision=maximum_precision).reshape(block_rows, model_width)
        blocks = lax.map(jax.checkpoint(one_block), jnp.arange(stream_count * block_count, dtype=jnp.int32))
        return blocks.reshape(stream_count, length, model_width)

    def forward(input_tokens, gain_one, query_key_value_weight, output_projection_weight, gain_two, up_projection_weight, down_projection_weight):
        normalized_input = low(layer_norm(input_tokens, gain_one))
        query_key_value = low_back(jnp.einsum('urh,hw->urw', normalized_input, query_key_value_weight, precision=maximum_precision))
        shape_heads = (stream_count, length, head_count, HEAD_DIM)
        queries = low(rotate(query_key_value[..., :model_width].reshape(shape_heads), angles))
        keys = low(rotate(query_key_value[..., model_width:2 * model_width].reshape(shape_heads), angles))
        values = low(query_key_value[..., 2 * model_width:].reshape(shape_heads))
        attention_output = low_back(low(attend(queries, keys, values)))
        residual_after_attention = input_tokens + low_back(jnp.einsum('urh,hw->urw', attention_output, output_projection_weight, precision=maximum_precision))
        second_normalized = low(layer_norm(residual_after_attention, gain_two))
        expanded_hidden = low_back(jnp.einsum('urh,hw->urw', second_normalized, up_projection_weight, precision=maximum_precision))
        gated_product = low(geglu(expanded_hidden[..., :hidden], expanded_hidden[..., hidden:]))
        return residual_after_attention + low_back(jnp.einsum('vwh,hj->vwj', gated_product, down_projection_weight, precision=maximum_precision))
    mixed, pullback = jax.vjp(forward, tokens.astype(jnp.float32), norm_gain.astype(jnp.float32), qkv_weight.astype(jnp.float32), proj_weight.astype(jnp.float32), ffn_gain.astype(jnp.float32), wide_weight.astype(jnp.float32), narrow_weight.astype(jnp.float32))
    grads = pullback(cotangent.astype(jnp.float32))
    return (mixed.astype(jnp.bfloat16), grads[0].astype(jnp.bfloat16), grads[1], grads[2], grads[3], grads[4], grads[5], grads[6])
```

```python
import math

import jax
import jax.numpy as jnp
from jax import lax
from jax.sharding import PartitionSpec as P

HEAD_DIM = 64
HALF_WIN = 64


eps_norm = 1e-05
mask_fill = -1e30


def extended(block, sides, width):
    for axis, dim in sides:
        count = lax.axis_size(axis)
        forward = [(i, i + 1) for i in range(count - 1)]
        backward = [(target, source) for source, target in forward]
        low = lax.ppermute(
            lax.slice_in_dim(block, block.shape[dim] - width, None, axis=dim), axis, forward
        )
        high = lax.ppermute(lax.slice_in_dim(block, 0, width, axis=dim), axis, backward)
        block = jnp.concatenate([low, block, high], axis=dim)
    return block


def layer_norm(values_in, gain_vec):
    centre_mean = jnp.mean(values_in, axis=-1, keepdims=True)
    centred = values_in - centre_mean
    variance = jnp.mean(centred * centred, axis=-1, keepdims=True)
    return centred * lax.rsqrt(variance + eps_norm) * gain_vec


def angle_table(positions, head_size):
    half_size = head_size // 2
    freqs = jnp.exp(
        jnp.arange(half_size, dtype=jnp.float32) * (-2.0 * math.log(10000.0) / head_size)
    )
    return positions.astype(jnp.float32)[..., None] * freqs


def rotate(tensor, angles):
    half_size = tensor.shape[-1] // 2
    cosine = jnp.cos(angles)[..., None, :]
    sine = jnp.sin(angles)[..., None, :]
    first_half = tensor[..., :half_size]
    second_half = tensor[..., half_size:]
    return jnp.concatenate(
        [first_half * cosine - second_half * sine, second_half * cosine + first_half * sine],
        axis=-1,
    )


def swap(block, axis, bit):
    count = lax.axis_size(axis)
    return lax.ppermute(block, axis, [(i, i ^ bit) for i in range(count)])


def pick(block, index, dim):
    return lax.dynamic_index_in_dim(block, index, dim, keepdims=False)


def halving(block, order, bits, last_type):
    me = lax.axis_index("seq")
    left = list(range(bits - 1, -1, -1))
    for step, bit in enumerate(order):
        dim = left.index(bit)
        left.pop(dim)
        mine = (me >> bit) & 1
        arrived = swap(pick(block, 1 - mine, dim), "seq", 1 << bit)
        kept = pick(block, mine, dim)
        block = kept.astype(jnp.float32) + arrived.astype(jnp.float32)
        block = block.astype(last_type if step + 1 == bits else arrived.dtype)
    return block


def bit_orders(bits):
    first = [0, 2, 1] if bits > 2 else list(range(bits))
    second = [1, 2, 0] if bits > 2 else list(range(bits))[::-1]
    rest = list(range(3, bits))
    return (first + rest, second + rest)


def turned_halves(left):
    seq_count, pair_count = lax.axis_size("seq"), lax.axis_size("fsdp")
    mine = lax.axis_index("fsdp")
    tokens_count, width = left.shape
    share = width // (seq_count * pair_count)
    turned = left.T.reshape(seq_count, pair_count, share, tokens_count)
    shape = (seq_count * share, tokens_count)
    return pick(turned, 1 - mine, 1).reshape(shape), pick(turned, mine, 1).reshape(shape)


def summed_grad(left, right):
    seq_count = lax.axis_size("seq")
    bits = seq_count.bit_length() - 1
    other, mine = turned_halves(left)
    columns = right.shape[1]
    middle = (columns // 2 + 127) // 128 * 128
    shares = []
    for part, order in zip((right[:, :middle], right[:, middle:]), bit_orders(bits)):
        sent = jnp.dot(other, part, preferred_element_type=jnp.float32).astype(jnp.bfloat16)
        arrived = swap(sent, "fsdp", 1)
        kept = jnp.dot(mine, part, preferred_element_type=jnp.float32)
        block = (kept + arrived.astype(jnp.float32)).astype(jnp.bfloat16)
        block = block.reshape((2,) * bits + (-1, part.shape[1]))
        shares.append(halving(block, order, bits, jnp.float32))
    return jnp.concatenate(shares, axis=1)


def geglu(gate_part, up_part):
    return jax.nn.gelu(gate_part, approximate=False) * up_part


def per_device(
    tokens,
    segment_ids,
    norm_gain,
    qkv_weight,
    proj_weight,
    ffn_gain,
    wide_weight,
    narrow_weight,
    cotangent,
):
    pair_me = lax.axis_index("fsdp")
    half_width = qkv_weight.shape[0]
    gains_own = jnp.stack([norm_gain, ffn_gain])
    qkv_other = swap(qkv_weight, "fsdp", 1)
    gains_other = swap(gains_own, "fsdp", 1)
    proj_other = swap(proj_weight, "fsdp", 1)
    wide_other = swap(wide_weight, "fsdp", 1)
    narrow_other = swap(narrow_weight, "fsdp", 1)

    def joined(own, other):
        return jnp.where(
            pair_me == 0,
            jnp.concatenate([own, other], axis=1),
            jnp.concatenate([other, own], axis=1),
        )

    def parted(block):
        return (
            lax.dynamic_slice_in_dim(block, pair_me * half_width, half_width, axis=1),
            lax.dynamic_slice_in_dim(block, (1 - pair_me) * half_width, half_width, axis=1),
        )

    def times_rows(block, own, other):
        block_own, block_other = parted(block)
        return jnp.dot(block_own, own, preferred_element_type=jnp.float32) + jnp.dot(
            block_other, other, preferred_element_type=jnp.float32
        )

    def times_turned(block, own, other):
        return joined(
            jnp.einsum("te,de->td", block, own, preferred_element_type=jnp.float32),
            jnp.einsum("te,de->td", block, other, preferred_element_type=jnp.float32),
        )

    gains = joined(gains_own, gains_other).astype(jnp.float32)
    gain_one = gains[0]
    gain_two = gains[1]
    rows_in = tokens[0]
    count_rows, model_width = rows_in.shape
    head_count = model_width // HEAD_DIM
    hidden = narrow_weight.shape[0]
    half_span = HALF_WIN
    ext_count = count_rows + 2 * half_span
    scale = HEAD_DIM ** (-0.5)
    stream_ids = segment_ids[0]
    length = stream_ids.shape[0]
    row_start = lax.axis_index("seq") * count_rows
    padded_ids = jnp.concatenate(
        [jnp.full((half_span,), -1, jnp.int32), stream_ids, jnp.full((half_span,), -2, jnp.int32)]
    )
    ext_ids = lax.dynamic_slice_in_dim(padded_ids, row_start, ext_count)
    ext_place = row_start - half_span + jnp.arange(ext_count, dtype=jnp.int32)
    first_of = jnp.sum((stream_ids[None, :] < ext_ids[:, None]).astype(jnp.int32), axis=1)
    ext_angles = angle_table(jnp.clip(ext_place, 0, length - 1) - first_of, HEAD_DIM)
    own_angles = ext_angles[half_span : half_span + count_rows]
    own_ids = ext_ids[half_span : half_span + count_rows]
    shape_heads = (count_rows, head_count, HEAD_DIM)
    rows_float = rows_in.astype(jnp.float32)
    normalized_input = layer_norm(rows_float, gain_one).astype(jnp.bfloat16)
    query_key_value = times_rows(normalized_input, qkv_weight, qkv_other)
    queries = rotate(query_key_value[:, :model_width].reshape(shape_heads), own_angles).astype(
        jnp.bfloat16
    )
    keys_own = rotate(
        query_key_value[:, model_width : 2 * model_width].reshape(shape_heads), own_angles
    ).astype(jnp.bfloat16)
    values_own = query_key_value[:, 2 * model_width :].astype(jnp.bfloat16)
    own_pair = jnp.concatenate([keys_own.reshape(count_rows, model_width), values_own], axis=1)
    ext_rows = extended(rows_in, (("seq", 0),), half_span)
    rim_rows = jnp.concatenate([ext_rows[:half_span], ext_rows[half_span + count_rows :]], axis=0)
    rim_angles = jnp.concatenate(
        [ext_angles[:half_span], ext_angles[half_span + count_rows :]], axis=0
    )
    rim_normed = layer_norm(rim_rows.astype(jnp.float32), gain_one).astype(jnp.bfloat16)
    rim_proj = times_rows(rim_normed, qkv_weight[:, model_width:], qkv_other[:, model_width:])
    rim_keys = rotate(
        rim_proj[:, :model_width].reshape(2 * half_span, head_count, HEAD_DIM), rim_angles
    ).astype(jnp.bfloat16)
    rim_pair = jnp.concatenate(
        [
            rim_keys.reshape(2 * half_span, model_width),
            rim_proj[:, model_width:].astype(jnp.bfloat16),
        ],
        axis=1,
    )
    ext_pair = jnp.concatenate([rim_pair[:half_span], own_pair, rim_pair[half_span:]], axis=0)
    ext_keys = ext_pair[:, :model_width].reshape(ext_count, head_count, HEAD_DIM)
    ext_values = ext_pair[:, model_width:].reshape(ext_count, head_count, HEAD_DIM)
    block_rows = count_rows
    key_span = block_rows + 2 * half_span

    def block_scores(block_index):
        base = block_index * block_rows
        query_place = row_start + base + jnp.arange(block_rows, dtype=jnp.int32)
        allowed = (jnp.abs(query_place[:, None] - ext_place[None, :]) <= half_span) & (
            own_ids[:, None] == ext_ids[None, :]
        )
        raw = (
            jnp.einsum("qhd,khd->hqk", queries, ext_keys, preferred_element_type=jnp.float32)
            * scale
        )
        return jnp.where(allowed[None], raw, mask_fill)

    block_index = 0
    base = block_index * block_rows
    scores = block_scores(block_index)
    row_top = jnp.max(scores, axis=-1, keepdims=True)
    raised = jnp.exp(scores - row_top)
    totals = jnp.sum(raised, axis=-1, keepdims=True)
    probs = raised / totals
    piece = jnp.einsum(
        "hqk,khd->qhd", probs.astype(jnp.bfloat16), ext_values, preferred_element_type=jnp.float32
    )
    pieces = piece.reshape(block_rows, model_width)
    attention_output = pieces.astype(jnp.bfloat16)
    residual_after_attention = rows_float + times_rows(attention_output, proj_weight, proj_other)
    second_normalized = layer_norm(residual_after_attention, gain_two).astype(jnp.bfloat16)
    expanded_hidden = times_rows(second_normalized, wide_weight, wide_other)
    gate = expanded_hidden[:, :hidden]
    up_part = expanded_hidden[:, hidden:]
    gated_product = geglu(gate, up_part).astype(jnp.bfloat16)
    final = residual_after_attention + joined(
        jnp.dot(gated_product, narrow_weight, preferred_element_type=jnp.float32),
        jnp.dot(gated_product, narrow_other, preferred_element_type=jnp.float32),
    )
    mixed = final.astype(jnp.bfloat16)[None]
    grad_out = cotangent[0].astype(jnp.float32)
    grad_low = cotangent[0]
    narrow_turned = summed_grad(grad_low, gated_product)
    low_own, low_other = parted(grad_low)
    grad_product = jnp.einsum(
        "td,fd->tf", low_own, narrow_weight, preferred_element_type=jnp.float32
    ) + jnp.einsum("td,fd->tf", low_other, narrow_other, preferred_element_type=jnp.float32)
    glu_pair, glu_back = jax.vjp(geglu, gate, up_part)
    grad_gate, grad_up = glu_back(grad_product)
    grad_wide = jnp.concatenate([grad_gate, grad_up], axis=1).astype(jnp.bfloat16)
    wide_g = summed_grad(second_normalized, grad_wide)
    grad_normed_two = times_turned(grad_wide, wide_weight, wide_other)
    norm_pair, second_back = jax.vjp(layer_norm, residual_after_attention, gain_two)
    grad_after_norm, ffn_gain_g = second_back(grad_normed_two)
    grad_after = grad_out + grad_after_norm
    grad_branch = grad_after.astype(jnp.bfloat16)
    proj_g = summed_grad(attention_output, grad_branch)
    grad_attended = times_turned(grad_branch, proj_weight, proj_other).astype(jnp.bfloat16)
    grad_attended = grad_attended.reshape(shape_heads)
    grad_probs = jnp.einsum(
        "qhd,khd->hqk", grad_attended, ext_values, preferred_element_type=jnp.float32
    )
    delta = jnp.sum(probs * grad_probs, axis=-1, keepdims=True)
    grad_scores = (probs * (grad_probs - delta)).astype(jnp.bfloat16)
    query_grads = (
        jnp.einsum("hqk,khd->qhd", grad_scores, ext_keys, preferred_element_type=jnp.float32)
        * scale
    )
    grad_keys = (
        jnp.einsum("hqk,qhd->khd", grad_scores, queries, preferred_element_type=jnp.float32) * scale
    )
    grad_values = jnp.einsum(
        "hqk,qhd->khd",
        probs.astype(jnp.bfloat16),
        grad_attended,
        preferred_element_type=jnp.float32,
    )
    grad_ext = jnp.concatenate(
        [grad_keys.reshape(key_span, model_width), grad_values.reshape(key_span, model_width)],
        axis=1,
    )
    rim_grads = jnp.concatenate([grad_ext[:half_span], grad_ext[half_span + count_rows :]], axis=0)
    arrived = extended(rim_grads.astype(jnp.bfloat16), (("seq", 0),), half_span).astype(
        rim_grads.dtype
    )
    own_grads = grad_ext[half_span : half_span + count_rows]
    blank = jnp.zeros((count_rows - half_span, 2 * model_width), jnp.float32)
    own_grads = (
        own_grads
        + jnp.concatenate([arrived[:half_span], blank], axis=0)
        + jnp.concatenate([blank, arrived[3 * half_span :]], axis=0)
    )
    grad_queries = rotate(query_grads, -own_angles).reshape(count_rows, model_width)
    grad_keys_raw = rotate(own_grads[:, :model_width].reshape(shape_heads), -own_angles).reshape(
        count_rows, model_width
    )
    grad_qkv = jnp.concatenate(
        [grad_queries, grad_keys_raw, own_grads[:, model_width:]], axis=1
    ).astype(jnp.bfloat16)
    qkv_g = summed_grad(normalized_input, grad_qkv)
    grad_normed = times_turned(grad_qkv, qkv_weight, qkv_other)
    first_pair, first_back = jax.vjp(layer_norm, rows_float, gain_one)
    grad_rows_norm, norm_gain_g = first_back(grad_normed)
    tokens_grad = (grad_after + grad_rows_norm).astype(jnp.bfloat16)[None]
    seq_count, pair_count = lax.axis_size("seq"), lax.axis_size("fsdp")
    bits = seq_count.bit_length() - 1
    both = jnp.stack([norm_gain_g, ffn_gain_g], axis=1).reshape(seq_count, pair_count, -1, 2)
    both = pick(both, pair_me, 1) + swap(pick(both, 1 - pair_me, 1), "fsdp", 1)
    both = halving(both.reshape((2,) * bits + (-1, 2)), list(range(bits)), bits, jnp.float32)
    return (
        mixed,
        tokens_grad,
        both[:, 0],
        qkv_g,
        proj_g,
        both[:, 1],
        wide_g,
        jnp.transpose(narrow_turned),
    )


def solution(mesh):
    return jax.shard_map(
        per_device,
        mesh=mesh,
        in_specs=(
            P("fsdp", "seq", None),
            P("fsdp", None),
            P("fsdp"),
            P("fsdp", None),
            P("fsdp", None),
            P("fsdp"),
            P("fsdp", None),
            P(None, "fsdp"),
            P("fsdp", "seq", None),
        ),
        out_specs=(
            P("fsdp", "seq", None),
            P("fsdp", "seq", None),
            P(("seq", "fsdp")),
            P(("seq", "fsdp"), None),
            P(("seq", "fsdp"), None),
            P(("seq", "fsdp")),
            P(("seq", "fsdp"), None),
            P(None, ("seq", "fsdp")),
        ),
        check_vma=False,
    )
```
